128 devices in a mesh: gx: 16 (over x, y_hi, core), gy: 8 (over y_lo, z).
Axes of the slice: x: 4, y: 4 (y_hi: 2, y_lo: 2; y = y_hi * 2 + y_lo), z: 4, core: 2. Of those that a mesh axis runs over, the one named last changes fastest.
Arguments:
- modes: float32 [3, 64, 32768], P(None, None, ('gx', 'gy')), may hold values from -6 to 6
- weights: float32 [32768], P(('gx', 'gy')), may hold values from 0.25 to 4
Outputs:
- tensor: float32 [64, 64, 64], P('gx', 'gy')
The draws below stay inside these ranges and needn't reach their ends.
All inputs are finite; a program needn't handle non-finite values.
Results may differ from the reference program's by a relative error of at most 0.00018.
Values sent between devices are 32-bit elements; how exact they have to be, the bound alone decides.
No kernel may reach another device: no remote copies, remote signals or barrier semaphores. Data moves between devices by JAX's collectives and lax.ppermute only.
A program may use at most 64 MiB of HBM per device.

```python
import math
import jax
import jax.numpy as jnp
from jax import lax

M = 64
NZ = 128
NX = 16
NY = 16
NCELLS = 32768


def steps_of(stream_key, shape, split, smallest, high):
    loudness, own = 1.0, jax.random.fold_in(stream_key, 6)
    for dim, shards_of in split:
        steps = jnp.exp(jax.random.uniform(jax.random.fold_in(own, dim), (shards_of,), jnp.float32, smallest / len(split), high / len(split)))
        loudness = loudness * jnp.repeat(steps, shape[dim] // shards_of).reshape([-1 if axis == dim else 1 for axis in range(len(shape))])
    return loudness


def bell_draw(key, shape, width, reach, split=(), kind=jnp.bfloat16):
    level = steps_of(key, shape, split, -0.22, 0.18) if split else 1.0
    values = jax.random.normal(key, shape, jnp.float32) * width * level
    return jnp.minimum(jnp.maximum(values, -reach), reach).astype(kind)


def setup_inputs(seed: int = 0) -> dict:
    key_list = jax.random.split(jax.random.key(seed), 3)
    return {
        "modes": bell_draw(key_list[0], (3, M, NCELLS), 1.0, 6.0, ((2, 128),), jnp.float32),
        "weights": jnp.clip(jnp.exp(math.log(4.0) - 2.7725887 * jax.random.uniform(key_list[1], (NCELLS,), jnp.float32) ** steps_of(key_list[1], (NCELLS,), ((0, 128),), -0.2, 0.2)), 0.25, 4.0),
    }


def differences(field, upper, lower):
    grad_x = (upper - lower) * 0.5
    grad_y = (jnp.roll(field, -1, axis=2) - jnp.roll(field, 1, axis=2)) * 0.5
    grad_z = (jnp.roll(field, -1, axis=3) - jnp.roll(field, 1, axis=3)) * 0.5
    return [grad_x, grad_y, grad_z]

def contribution(field, grads, weighted):
    weighted_field = field * weighted
    result = jnp.zeros((field.shape[1], field.shape[1], field.shape[1]), jnp.float32)
    for comp_a in range(3):
        inner = field[0][:, None, :] * grads[0][comp_a][None, :, :]
        inner = inner + field[1][:, None, :] * grads[1][comp_a][None, :, :]
        inner = inner + field[2][:, None, :] * grads[2][comp_a][None, :, :]
        result = result + jnp.einsum('ic,jkc->ijk', weighted_field[comp_a], inner, precision=lax.Precision.HIGHEST)
    return result

def reference(modes, weights):
    mode_count = modes.shape[1]
    grid = modes.reshape(3, mode_count, NZ, NY, NX).transpose(0, 1, 4, 3, 2)
    weight_grid = weights.reshape(NZ, NY, NX).transpose(2, 1, 0)
    factor = 1.0 / math.sqrt(NX * NY * NZ)
    padded = jnp.concatenate([grid[:, :, -1:], grid, grid[:, :, :1]], axis=2)

    def plane(total, position):
        slab = lax.dynamic_slice_in_dim(padded, position, 3, axis=2)
        field = slab[:, :, 1]
        grads = differences(field, slab[:, :, 2], slab[:, :, 0])
        weight_row = lax.dynamic_index_in_dim(weight_grid, position, 0, keepdims=False) * factor
        flat = field.reshape(3, mode_count, -1)
        flat_grads = [g.reshape(3, mode_count, -1) for g in grads]
        return (total + contribution(flat, flat_grads, weight_row.reshape(-1)), None)
    total, _ = lax.scan(plane, jnp.zeros((mode_count, mode_count, mode_count), jnp.float32), jnp.arange(NX, dtype=jnp.int32))
    return total
```

```python
import functools
import math

import numpy as np
import jax
import jax.numpy as jnp
from jax import lax
from jax.experimental import pallas as pl
from jax.experimental.pallas import tpu as pltpu
from jax.sharding import Mesh, PartitionSpec as P

NX = 16
PARTS = ("x", "yh", "c", "yl", "z")
CHIPS = ("x", "yh", "yl", "z")
F32 = jnp.float32
BF16 = jnp.bfloat16


def halves(value):
    high = value.astype(BF16)
    low = (value - high.astype(F32)).astype(BF16)
    return high, low


def stacked_halves(value):
    high, low = halves(value)
    return jnp.concatenate([high, low], axis=0)


def block_product(rows, grads, stacked):
    modes = grads[0].shape[0]
    pieces = []
    for i in range(4):
        inner = rows[i : i + 1] * grads[0]
        inner = inner + rows[4 + i : 5 + i] * grads[1]
        inner = inner + rows[8 + i : 9 + i] * grads[2]
        pieces.append(inner)
    high, low = halves(jnp.concatenate(pieces, axis=0))
    dims = (((1,), (1,)), ((), ()))
    both = lax.dot_general(stacked, high, dims, preferred_element_type=F32)
    rest = lax.dot_general(stacked[:modes], low, dims, preferred_element_type=F32)
    return both[:modes] + both[modes:] + rest


def plane_kernel(scale, modes_ref, weights_ref, out_ref, rows_ref, grad_ref, stack_ref):
    cells = modes_ref.shape[2]
    weight = weights_ref[...] * scale
    lane = lax.broadcasted_iota(jnp.int32, modes_ref.shape[1:], 1) % NX
    for a in range(3):
        field = modes_ref[a]
        weighted = field * weight
        for block in range(16):
            rows_ref[block, 4 * a : 4 * a + 4, :] = weighted[4 * block : 4 * block + 4]
        after = jnp.where(lane == NX - 1, pltpu.roll(field, NX - 1, 1), pltpu.roll(field, cells - 1, 1))
        before = jnp.where(lane == 0, pltpu.roll(field, cells - (NX - 1), 1), pltpu.roll(field, 1, 1))
        grad_ref[0, a] = (after - before) * 0.5
        grad_ref[1, a] = (pltpu.roll(field, cells - NX, 1) - pltpu.roll(field, NX, 1)) * 0.5
        if a < 2:
            stack_ref[a] = stacked_halves(field)

    def body(block, _):
        rows = rows_ref[block]
        total = None
        for b in range(2):
            part = block_product(rows, [grad_ref[b, 0], grad_ref[b, 1], grad_ref[b, 2]], stack_ref[b])
            total = part if total is None else total + part
        for j in range(8):
            for h in range(2):
                out_ref[block % 2, (block // 2) * 8 + j, 8 * h : 8 * h + 8, :] = total[
                    8 * j : 8 * j + 8, 128 * h : 128 * h + 128
                ]
        return 0

    lax.fori_loop(0, 16, body, 0)


def normal_kernel(half_ref, field_ref, after_ref, before_ref, rows_ref, partial_ref, out_ref, grad_ref, stack_ref):
    half = half_ref[0]
    for a in range(3):
        grad_ref[a] = (after_ref[a] - before_ref[a]) * 0.5
    stack_ref[...] = stacked_halves(field_ref[2])

    def body(block, _):
        rows = rows_ref[2 * block + half]
        total = block_product(rows, [grad_ref[0], grad_ref[1], grad_ref[2]], stack_ref[...])
        for j in range(8):
            for h in range(2):
                at = block * 8 + j
                out_ref[at, 8 * h : 8 * h + 8, :] = (
                    partial_ref[half, at, 8 * h : 8 * h + 8, :]
                    + total[8 * j : 8 * j + 8, 128 * h : 128 * h + 128]
                )
        return 0

    lax.fori_loop(0, 8, body, 0)


def final_kernel(blocks_ref, out_ref):
    total = jnp.sum(blocks_ref[...], axis=0)
    for h in range(2):
        rows = total[8 * h : 8 * h + 8]
        out_ref[2 * h] = rows[:, :64]
        out_ref[2 * h + 1] = rows[:, 64:]


VM = pl.BlockSpec(memory_space=pltpu.VMEM)
SM = pl.BlockSpec(memory_space=pltpu.SMEM)


def per_device(modes, weights, *, count):
    cells = modes.shape[2]
    factor = 1.0 / math.sqrt(count * cells)
    up = [(i, (i + 1) % count) for i in range(count)]
    before = lax.ppermute(modes, PARTS, up)
    after = lax.ppermute(modes, PARTS, [(b, a) for a, b in up])

    shape = jax.ShapeDtypeStruct
    local = lambda array: pltpu.with_memory_space_constraint(array, pltpu.VMEM)
    field = local(modes)
    partial, rows = pl.pallas_call(
        functools.partial(plane_kernel, factor),
        out_shape=[pltpu.VMEM((2, 64, 16, 128), F32), pltpu.VMEM((16, 12, cells), F32)],
        in_specs=[VM, VM],
        out_specs=[VM, VM],
        scratch_shapes=[pltpu.VMEM((2, 3, 64, cells), F32), pltpu.VMEM((2, 128, cells), BF16)],
        name="plane",
    )(field, weights.reshape(1, cells))

    core = lax.axis_index("c").astype(jnp.int32)
    half_call = pl.pallas_call(
        normal_kernel,
        out_shape=pltpu.VMEM((64, 16, 128), F32),
        in_specs=[SM, VM, VM, VM, VM, VM],
        out_specs=VM,
        scratch_shapes=[pltpu.VMEM((3, 64, cells), F32), pltpu.VMEM((128, cells), BF16)],
        name="normal",
    )
    after, before, rows, partial = local(after), local(before), local(rows), local(partial)
    theirs = half_call((1 - core)[None], field, after, before, rows, partial)
    arrived = lax.ppermute(theirs, "c", [(0, 1), (1, 0)])
    mine = half_call(core[None], field, after, before, rows, partial)
    blocks = mine + arrived
    gathered = lax.all_to_all(blocks, CHIPS, split_axis=0, concat_axis=0, tiled=True)
    return pl.pallas_call(
        final_kernel, out_shape=shape((4, 8, 64), F32), in_specs=[VM], out_specs=VM, name="final"
    )(local(gathered))


def solution(mesh):
    fine = Mesh(np.asarray(mesh.devices).reshape(4, 2, 2, 2, 4), PARTS)
    return jax.shard_map(
        functools.partial(per_device, count=mesh.devices.size),
        mesh=fine,
        in_specs=(P(None, None, PARTS), P(PARTS)),
        out_specs=P(("x", "yh", "c"), ("yl", "z"), None),
        check_vma=False,
    )
```

```python
import functools
import math

import numpy as np
import jax
import jax.numpy as jnp
from jax import lax
from jax.experimental import pallas as pl
from jax.experimental.pallas import tpu as pltpu
from jax.sharding import Mesh, PartitionSpec as P

NX = 16
PARTS = ("x", "yh", "c", "yl", "z")
CHIPS = ("x", "yh", "yl", "z")
F32 = jnp.float32
BF16 = jnp.bfloat16


def halves(value):
    high = value.astype(BF16)
    low = (value - high.astype(F32)).astype(BF16)
    return high, low


def stacked_halves(value):
    high, low = halves(value)
    return jnp.concatenate([high, low], axis=0)


def block_product(rows, grads, stacked):
    modes = grads[0].shape[0]
    pieces = []
    for i in range(4):
        inner = rows[i : i + 1] * grads[0]
        inner = inner + rows[4 + i : 5 + i] * grads[1]
        inner = inner + rows[8 + i : 9 + i] * grads[2]
        pieces.append(inner)
    high, low = halves(jnp.concatenate(pieces, axis=0))
    dims = (((1,), (1,)), ((), ()))
    both = lax.dot_general(stacked, high, dims, preferred_element_type=F32)
    rest = lax.dot_general(stacked[:modes], low, dims, preferred_element_type=F32)
    return both[:modes] + both[modes:] + rest


def weighted_rows(rows_ref, field, weight, a):
    weighted = field * weight
    for block in range(16):
        rows_ref[block, 4 * a : 4 * a + 4, :] = weighted[4 * block : 4 * block + 4]


def components(ref, *at):
    return [ref[(*at, a)] for a in range(3)]


def tile(block, j, h):
    return block * 8 + j, slice(8 * h, 8 * h + 8), (slice(8 * j, 8 * j + 8), slice(128 * h, 128 * h + 128))


def plane_blocks(half, rows_ref, grad_ref, stack_ref, out_ref):
    for block in range(8):
        rows = rows_ref[2 * block + half]
        total = block_product(rows, components(grad_ref, 0), stack_ref[0])
        total = total + block_product(rows, components(grad_ref, 1), stack_ref[1])
        for j in range(8):
            for h in range(2):
                at, sub, part = tile(block, j, h)
                out_ref[at, sub, :] = total[part]


def first_plane_kernel(scale, modes_ref, weights_ref, out_ref, rows_ref, scaled_ref, grad_ref, stack_ref):
    cells = modes_ref.shape[2]
    weight = weights_ref[...] * scale
    scaled_ref[...] = weight
    lane = lax.broadcasted_iota(jnp.int32, modes_ref.shape[1:], 1) % NX
    for a in range(3):
        field = modes_ref[a]
        weighted_rows(rows_ref, field, weight, a)
        after = jnp.where(lane == NX - 1, pltpu.roll(field, NX - 1, 1), pltpu.roll(field, cells - 1, 1))
        before = jnp.where(lane == 0, pltpu.roll(field, cells - (NX - 1), 1), pltpu.roll(field, 1, 1))
        grad_ref[0, a] = after - before
        grad_ref[1, a] = pltpu.roll(field, cells - NX, 1) - pltpu.roll(field, NX, 1)
        stack_ref[a] = stacked_halves(-field if a == 2 else field)
    plane_blocks(1 - lax.axis_index("c"), rows_ref, grad_ref, stack_ref, out_ref)


def second_plane_kernel(rows_ref, grad_ref, stack_ref, out_ref):
    plane_blocks(lax.axis_index("c"), rows_ref, grad_ref, stack_ref, out_ref)


def edge_blocks(half, field_ref, below_ref, rows_ref, low_rows_ref, stack_ref, low_stack_ref, partial_ref, out_ref):
    for block in range(8):
        total = block_product(rows_ref[2 * block + half], components(below_ref), stack_ref[2])
        total = total + block_product(low_rows_ref[2 * block + half], components(field_ref), low_stack_ref[...])
        for j in range(8):
            for h in range(2):
                at, sub, part = tile(block, j, h)
                out_ref[at, sub, :] = partial_ref[at, sub, :] + total[part]


def first_edge_kernel(
    field_ref, below_ref, weight_ref, rows_ref, stack_ref, partial_ref, out_ref, low_rows_ref, low_stack_ref
):
    for a in range(3):
        weighted_rows(low_rows_ref, below_ref[a], weight_ref[...], a)
    low_stack_ref[...] = stacked_halves(below_ref[2])
    half = 1 - lax.axis_index("c")
    edge_blocks(half, field_ref, below_ref, rows_ref, low_rows_ref, stack_ref, low_stack_ref, partial_ref, out_ref)


def second_edge_kernel(
    field_ref, below_ref, rows_ref, stack_ref, partial_ref, low_rows_ref, low_stack_ref, out_ref
):
    half = lax.axis_index("c")
    edge_blocks(half, field_ref, below_ref, rows_ref, low_rows_ref, stack_ref, low_stack_ref, partial_ref, out_ref)


def final_kernel(blocks_ref, out_ref):
    total = jnp.sum(blocks_ref[...], axis=0)
    for h in range(2):
        rows = total[8 * h : 8 * h + 8]
        out_ref[2 * h] = rows[:, :64]
        out_ref[2 * h + 1] = rows[:, 64:]


LIMIT = 12 << 20
VM = pl.BlockSpec(memory_space=pltpu.VMEM)


def local_call(kernel, name, outs, *args):
    args = [pltpu.with_memory_space_constraint(arg, pltpu.VMEM) for arg in args]
    return pl.pallas_call(
        kernel,
        out_shape=[pltpu.VMEM(shape, kind) for shape, kind in outs],
        in_specs=[VM] * len(args),
        out_specs=[VM] * len(outs),
        compiler_params=pltpu.CompilerParams(vmem_limit_bytes=LIMIT),
        name=name,
    )(*args)


def per_device(modes, weights, *, count):
    cells = modes.shape[2]
    factor = 0.5 / math.sqrt(count * cells)
    up = [(i, (i + 1) % count) for i in range(count)]
    below = lax.ppermute(modes, PARTS, up)

    blocks = ((64, 16, 128), F32)
    rows_shape = ((16, 12, cells), F32)
    field = pltpu.with_memory_space_constraint(modes, pltpu.VMEM)
    theirs, rows, scaled, grad, stack = local_call(
        functools.partial(first_plane_kernel, factor),
        "plane_theirs",
        [blocks, rows_shape, ((1, cells), F32), ((2, 3, 64, cells), F32), ((3, 128, cells), BF16)],
        field,
        weights.reshape(1, cells),
    )
    below_weight = lax.ppermute(scaled, PARTS, up)
    (mine,) = local_call(second_plane_kernel, "plane_mine", [blocks], rows, grad, stack)
    below, mine = lax.optimization_barrier((below, mine))
    theirs, low_rows, low_stack = local_call(
        first_edge_kernel,
        "edge_theirs",
        [blocks, rows_shape, ((128, cells), BF16)],
        field,
        below,
        below_weight,
        rows,
        stack,
        theirs,
    )
    arrived = lax.ppermute(theirs, "c", [(0, 1), (1, 0)])
    (mine,) = local_call(
        second_edge_kernel, "edge_mine", [blocks], field, below, rows, stack, mine, low_rows, low_stack
    )
    gathered = lax.all_to_all(mine + arrived, CHIPS, split_axis=0, concat_axis=0, tiled=True)
    return pl.pallas_call(
        final_kernel, out_shape=jax.ShapeDtypeStruct((4, 8, 64), F32), in_specs=[VM], out_specs=VM, name="final"
    )(pltpu.with_memory_space_constraint(gathered, pltpu.VMEM))


def solution(mesh):
    fine = Mesh(np.asarray(mesh.devices).reshape(4, 2, 2, 2, 4), PARTS)
    return jax.shard_map(
        functools.partial(per_device, count=mesh.devices.size),
        mesh=fine,
        in_specs=(P(None, None, PARTS), P(PARTS)),
        out_specs=P(("x", "yh", "c"), ("yl", "z"), None),
        check_vma=False,
    )
```

```python
import functools
import math

import numpy as np
import jax
import jax.numpy as jnp
from jax import lax
from jax.experimental import pallas as pl
from jax.experimental.pallas import tpu as pltpu
from jax.sharding import Mesh, PartitionSpec as P

NX = 16
PARTS = ("x", "yh", "c", "yl", "z")
CHIPS = ("x", "yh", "yl", "z")
F32 = jnp.float32
BF16 = jnp.bfloat16


def halves(value):
    high = value.astype(BF16)
    low = (value - high.astype(F32)).astype(BF16)
    return high, low


def stacked_halves(value):
    high, low = halves(value)
    return jnp.concatenate([high, low], axis=0)


def block_product(rows, grads, stacked):
    modes = grads[0].shape[0]
    pieces = []
    for i in range(4):
        inner = rows[i : i + 1] * grads[0]
        inner = inner + rows[4 + i : 5 + i] * grads[1]
        inner = inner + rows[8 + i : 9 + i] * grads[2]
        pieces.append(inner)
    high, low = halves(jnp.concatenate(pieces, axis=0))
    dims = (((1,), (1,)), ((), ()))
    both = lax.dot_general(stacked, high, dims, preferred_element_type=F32)
    rest = lax.dot_general(stacked[:modes], low, dims, preferred_element_type=F32)
    return both[:modes] + both[modes:] + rest


def weighted_rows(rows_ref, field, weight, a):
    weighted = field * weight
    for block in range(16):
        rows_ref[block, 4 * a : 4 * a + 4, :] = weighted[4 * block : 4 * block + 4]


def components(ref, *at):
    return [ref[(*at, a)] for a in range(3)]


def tile(block, j, h):
    return block * 8 + j, slice(8 * h, 8 * h + 8), (slice(8 * j, 8 * j + 8), slice(128 * h, 128 * h + 128))


def plane_blocks(half, rows_ref, grad_ref, stack_ref, out_ref):
    for block in range(8):
        rows = rows_ref[2 * block + half]
        total = block_product(rows, components(grad_ref, 0), stack_ref[0])
        total = total + block_product(rows, components(grad_ref, 1), stack_ref[1])
        for j in range(8):
            for h in range(2):
                at, sub, part = tile(block, j, h)
                out_ref[at, sub, :] = total[part]


def plane_kernel(
    scale, modes_ref, weights_ref, theirs_ref, mine_ref, rows_ref, field_ref, edge_stack_ref, weight_ref, grad_ref, stack_ref, sems
):
    fetches = [pltpu.make_async_copy(weights_ref, weight_ref, sems.at[3])]
    fetches += [pltpu.make_async_copy(modes_ref.at[a], field_ref.at[a], sems.at[a]) for a in range(3)]
    for fetch in fetches:
        fetch.start()
    cells = field_ref.shape[2]
    lane = lax.broadcasted_iota(jnp.int32, field_ref.shape[1:], 1) % NX
    fetches[0].wait()
    weight = weight_ref[...] * scale
    for a in range(3):
        fetches[1 + a].wait()
        field = field_ref[a]
        weighted_rows(rows_ref, field, weight, a)
        after = jnp.where(lane == NX - 1, pltpu.roll(field, NX - 1, 1), pltpu.roll(field, cells - 1, 1))
        before = jnp.where(lane == 0, pltpu.roll(field, cells - (NX - 1), 1), pltpu.roll(field, 1, 1))
        grad_ref[0, a] = after - before
        grad_ref[1, a] = pltpu.roll(field, cells - NX, 1) - pltpu.roll(field, NX, 1)
        if a < 2:
            stack_ref[a] = stacked_halves(field)
        else:
            edge_stack_ref[...] = stacked_halves(-field)
    core = lax.axis_index("c")
    plane_blocks(1 - core, rows_ref, grad_ref, stack_ref, theirs_ref)
    plane_blocks(core, rows_ref, grad_ref, stack_ref, mine_ref)


def edge_blocks(half, field_ref, below_ref, rows_ref, low_rows_ref, stack_ref, low_stack_ref, partial_ref, out_ref):
    for block in range(8):
        total = block_product(rows_ref[2 * block + half], components(below_ref), stack_ref[...])
        total = total + block_product(low_rows_ref[2 * block + half], components(field_ref), low_stack_ref[...])
        for j in range(8):
            for h in range(2):
                at, sub, part = tile(block, j, h)
                out_ref[at, sub, :] = partial_ref[at, sub, :] + total[part]


def first_edge_kernel(
    scale, field_ref, below_ref, weight_ref, rows_ref, stack_ref, partial_ref, out_ref, low_rows_ref, low_stack_ref
):
    weight = weight_ref[...] * scale
    for a in range(3):
        weighted_rows(low_rows_ref, below_ref[a], weight, a)
    low_stack_ref[...] = stacked_halves(below_ref[2])
    half = 1 - lax.axis_index("c")
    edge_blocks(half, field_ref, below_ref, rows_ref, low_rows_ref, stack_ref, low_stack_ref, partial_ref, out_ref)


def second_edge_kernel(
    field_ref, below_ref, rows_ref, stack_ref, partial_ref, low_rows_ref, low_stack_ref, out_ref
):
    half = lax.axis_index("c")
    edge_blocks(half, field_ref, below_ref, rows_ref, low_rows_ref, stack_ref, low_stack_ref, partial_ref, out_ref)


def final_kernel(blocks_ref, out_ref):
    total = jnp.sum(blocks_ref[...], axis=0)
    for h in range(2):
        rows = total[8 * h : 8 * h + 8]
        out_ref[2 * h] = rows[:, :64]
        out_ref[2 * h + 1] = rows[:, 64:]


LIMIT = 12 << 20
VM = pl.BlockSpec(memory_space=pltpu.VMEM)


HBM = pl.BlockSpec(memory_space=pltpu.HBM)


def local_call(kernel, name, outs, *args, scratch=(), spec=VM):
    args = [pltpu.with_memory_space_constraint(arg, spec.memory_space) for arg in args]
    return pl.pallas_call(
        kernel,
        out_shape=[pltpu.VMEM(shape, kind) for shape, kind in outs],
        in_specs=[spec] * len(args),
        out_specs=[VM] * len(outs),
        scratch_shapes=scratch,
        compiler_params=pltpu.CompilerParams(vmem_limit_bytes=LIMIT),
        name=name,
    )(*args)


def per_device(modes, weights, *, count):
    cells = modes.shape[2]
    factor = 0.5 / math.sqrt(count * cells)
    up = [(i, (i + 1) % count) for i in range(count)]
    weights = weights.reshape(1, cells)
    below = lax.ppermute(modes, PARTS, up)
    below_weight = lax.ppermute(weights, PARTS, up)

    blocks = ((64, 16, 128), F32)
    rows_shape = ((16, 12, cells), F32)
    theirs, mine, rows, field, stack = local_call(
        functools.partial(plane_kernel, factor),
        "plane",
        [blocks, blocks, rows_shape, ((3, 64, cells), F32), ((128, cells), BF16)],
        modes,
        weights,
        scratch=[
            pltpu.VMEM((1, cells), F32),
            pltpu.VMEM((2, 3, 64, cells), F32),
            pltpu.VMEM((2, 128, cells), BF16),
            pltpu.SemaphoreType.DMA((4,)),
        ],
        spec=HBM,
    )
    theirs, low_rows, low_stack = local_call(
        functools.partial(first_edge_kernel, factor),
        "edge_theirs",
        [blocks, rows_shape, ((128, cells), BF16)],
        field,
        below,
        below_weight,
        rows,
        stack,
        theirs,
    )
    arrived = lax.ppermute(theirs, "c", [(0, 1), (1, 0)])
    (mine,) = local_call(
        second_edge_kernel, "edge_mine", [blocks], field, below, rows, stack, mine, low_rows, low_stack
    )
    gathered = lax.all_to_all(mine + arrived, CHIPS, split_axis=0, concat_axis=0, tiled=True)
    return pl.pallas_call(
        final_kernel, out_shape=jax.ShapeDtypeStruct((4, 8, 64), F32), in_specs=[VM], out_specs=VM, name="final"
    )(pltpu.with_memory_space_constraint(gathered, pltpu.VMEM))


def solution(mesh):
    fine = Mesh(np.asarray(mesh.devices).reshape(4, 2, 2, 2, 4), PARTS)
    return jax.shard_map(
        functools.partial(per_device, count=mesh.devices.size),
        mesh=fine,
        in_specs=(P(None, None, PARTS), P(PARTS)),
        out_specs=P(("x", "yh", "c"), ("yl", "z"), None),
        check_vma=False,
    )
```

```python
import functools
import math

import numpy as np
import jax
import jax.numpy as jnp
from jax import lax
from jax.experimental import pallas as pl
from jax.experimental.pallas import tpu as pltpu
from jax.sharding import Mesh, PartitionSpec as P

NX = 16
PARTS = ("x", "yh", "c", "yl", "z")
CHIPS = ("x", "yh", "yl", "z")
F32 = jnp.float32
BF16 = jnp.bfloat16


def halves(value):
    high = value.astype(BF16)
    low = (value - high.astype(F32)).astype(BF16)
    return high, low


def stationary(field):
    tall = jnp.concatenate([field, field], axis=0).T
    high = tall.astype(BF16).astype(F32)
    first = lax.broadcasted_iota(jnp.int32, tall.shape, 1) < field.shape[0]
    return jnp.where(first, high, tall - high).astype(BF16)


def block_product(rows, grads, right):
    pieces = []
    for i in range(4):
        inner = rows[i : i + 1] * grads[0]
        inner = inner + rows[4 + i : 5 + i] * grads[1]
        inner = inner + rows[8 + i : 9 + i] * grads[2]
        pieces.append(inner)
    high, low = halves(jnp.concatenate(pieces, axis=0))
    both = jnp.dot(jnp.concatenate([high, low], axis=0), right, preferred_element_type=F32)
    return both[:256] + both[256:]


def messages(total):
    for pair in range(2):
        turned = total[128 * pair : 128 * pair + 128].T
        yield pair, turned[:64] + turned[64:]


def weighted_rows(rows_ref, field, weight, a):
    weighted = field * weight
    for block in range(16):
        rows_ref[block, 4 * a : 4 * a + 4, :] = weighted[4 * block : 4 * block + 4]


def components(ref, *at):
    return [ref[(*at, a)] for a in range(3)]


def plane_blocks(half, rows_ref, grad_ref, right_ref, out_ref):
    for block in range(8):
        rows = rows_ref[2 * block + half]
        total = block_product(rows, components(grad_ref, 0), right_ref[0])
        total = total + block_product(rows, components(grad_ref, 1), right_ref[1])
        for pair, sums in messages(total):
            for j in range(8):
                out_ref[8 * block + j, 8 * pair : 8 * pair + 8, :] = sums[8 * j : 8 * j + 8]


def plane_kernel(
    scale, modes_ref, weights_ref, theirs_ref, mine_ref, rows_ref, field_ref, edge_right_ref, weight_ref, grad_ref, right_ref, sems
):
    fetches = [pltpu.make_async_copy(weights_ref, weight_ref, sems.at[3])]
    fetches += [pltpu.make_async_copy(modes_ref.at[a], field_ref.at[a], sems.at[a]) for a in range(3)]
    for fetch in fetches:
        fetch.start()
    cells = field_ref.shape[2]
    lane = lax.broadcasted_iota(jnp.int32, field_ref.shape[1:], 1) % NX
    fetches[0].wait()
    weight = weight_ref[...] * scale
    for a in range(3):
        fetches[1 + a].wait()
        field = field_ref[a]
        weighted_rows(rows_ref, field, weight, a)
        after = jnp.where(lane == NX - 1, pltpu.roll(field, NX - 1, 1), pltpu.roll(field, cells - 1, 1))
        before = jnp.where(lane == 0, pltpu.roll(field, cells - (NX - 1), 1), pltpu.roll(field, 1, 1))
        grad_ref[0, a] = after - before
        grad_ref[1, a] = pltpu.roll(field, cells - NX, 1) - pltpu.roll(field, NX, 1)
        if a < 2:
            right_ref[a] = stationary(field)
        else:
            edge_right_ref[...] = stationary(field)
    core = lax.axis_index("c")
    plane_blocks(1 - core, rows_ref, grad_ref, right_ref, theirs_ref)
    plane_blocks(core, rows_ref, grad_ref, right_ref, mine_ref)


def edge_blocks(half, slope_ref, rows_ref, low_rows_ref, right_ref, low_right_ref, partial_ref, out_ref):
    slopes = components(slope_ref)
    for block in range(8):
        total = block_product(rows_ref[2 * block + half], slopes, right_ref[...])
        total = total + block_product(low_rows_ref[2 * block + half], slopes, low_right_ref[...])
        for pair, sums in messages(total):
            for j in range(8):
                at, sub = 8 * block + j, slice(8 * pair, 8 * pair + 8)
                out_ref[at, sub, :] = partial_ref[at, sub, :] + sums[8 * j : 8 * j + 8]


def first_edge_kernel(
    scale, field_ref, below_ref, weight_ref, rows_ref, right_ref, partial_ref, out_ref, slope_ref, low_rows_ref, low_right_ref
):
    weight = weight_ref[...] * scale
    for a in range(3):
        slope_ref[a] = field_ref[a] - below_ref[a]
        weighted_rows(low_rows_ref, below_ref[a], weight, a)
    low_right_ref[...] = stationary(below_ref[2])
    half = 1 - lax.axis_index("c")
    edge_blocks(half, slope_ref, rows_ref, low_rows_ref, right_ref, low_right_ref, partial_ref, out_ref)


def second_edge_kernel(slope_ref, rows_ref, low_rows_ref, right_ref, low_right_ref, partial_ref, out_ref):
    half = lax.axis_index("c")
    edge_blocks(half, slope_ref, rows_ref, low_rows_ref, right_ref, low_right_ref, partial_ref, out_ref)


def final_kernel(blocks_ref, out_ref):
    total = jnp.sum(blocks_ref[...], axis=0)
    for h in range(2):
        rows = total[8 * h : 8 * h + 8]
        out_ref[2 * h] = rows[:, :64]
        out_ref[2 * h + 1] = rows[:, 64:]


LIMIT = 12 << 20
VM = pl.BlockSpec(memory_space=pltpu.VMEM)


HBM = pl.BlockSpec(memory_space=pltpu.HBM)


def local_call(kernel, name, outs, *args, scratch=(), spec=VM):
    args = [pltpu.with_memory_space_constraint(arg, spec.memory_space) for arg in args]
    return pl.pallas_call(
        kernel,
        out_shape=[pltpu.VMEM(shape, kind) for shape, kind in outs],
        in_specs=[spec] * len(args),
        out_specs=[VM] * len(outs),
        scratch_shapes=scratch,
        compiler_params=pltpu.CompilerParams(vmem_limit_bytes=LIMIT),
        name=name,
    )(*args)


def per_device(modes, weights, *, count):
    cells = modes.shape[2]
    factor = 0.5 / math.sqrt(count * cells)
    up = [(i, (i + 1) % count) for i in range(count)]
    weights = weights.reshape(1, cells)
    below = lax.ppermute(modes, PARTS, up)
    below_weight = lax.ppermute(weights, PARTS, up)

    blocks = ((64, 16, 128), F32)
    rows_shape = ((16, 12, cells), F32)
    plane = ((3, 64, cells), F32)
    right_shape = ((cells, 128), BF16)
    theirs, mine, rows, field, right = local_call(
        functools.partial(plane_kernel, factor),
        "plane",
        [blocks, blocks, rows_shape, plane, right_shape],
        modes,
        weights,
        scratch=[
            pltpu.VMEM((1, cells), F32),
            pltpu.VMEM((2, 3, 64, cells), F32),
            pltpu.VMEM((2, cells, 128), BF16),
            pltpu.SemaphoreType.DMA((4,)),
        ],
        spec=HBM,
    )
    theirs, slope, low_rows, low_right = local_call(
        functools.partial(first_edge_kernel, factor),
        "edge_theirs",
        [blocks, plane, rows_shape, right_shape],
        field,
        below,
        below_weight,
        rows,
        right,
        theirs,
    )
    arrived = lax.ppermute(theirs, PARTS, [(i, i ^ 8) for i in range(count)])
    (mine,) = local_call(
        second_edge_kernel, "edge_mine", [blocks], slope, rows, low_rows, right, low_right, mine
    )
    gathered = lax.all_to_all(mine + arrived, CHIPS, split_axis=0, concat_axis=0, tiled=True)
    return pl.pallas_call(
        final_kernel, out_shape=jax.ShapeDtypeStruct((4, 8, 64), F32), in_specs=[VM], out_specs=VM, name="final"
    )(pltpu.with_memory_space_constraint(gathered, pltpu.VMEM))


def solution(mesh):
    fine = Mesh(np.asarray(mesh.devices).reshape(4, 2, 2, 2, 4), PARTS)
    return jax.shard_map(
        functools.partial(per_device, count=mesh.devices.size),
        mesh=fine,
        in_specs=(P(None, None, PARTS), P(PARTS)),
        out_specs=P(("x", "yh", "c"), ("yl", "z"), None),
        check_vma=False,
    )
```

```python
import functools
import math

import numpy as np
import jax
import jax.numpy as jnp
from jax import lax
from jax.experimental import pallas as pl
from jax.experimental.pallas import tpu as pltpu
from jax.sharding import Mesh, PartitionSpec as P

NX = 16
PARTS = ("x", "yh", "c", "yl", "z")
CHIPS = ("x", "yh", "yl", "z")
F32 = jnp.float32
BF16 = jnp.bfloat16


def halves(value):
    high = value.astype(BF16)
    low = (value - high.astype(F32)).astype(BF16)
    return high, low


def stationary(field):
    tall = jnp.concatenate([field, field], axis=0).T
    high = tall.astype(BF16).astype(F32)
    first = lax.broadcasted_iota(jnp.int32, tall.shape, 1) < field.shape[0]
    return jnp.where(first, high, tall - high).astype(BF16)


def products(rows, grads):
    pieces = []
    for i in range(4):
        inner = rows[i : i + 1] * grads[0]
        inner = inner + rows[4 + i : 5 + i] * grads[1]
        inner = inner + rows[8 + i : 9 + i] * grads[2]
        pieces.append(inner)
    return halves(jnp.concatenate(pieces, axis=0))


def block_sums(many, grads, right):
    highs, lows = zip(*[products(rows, grads) for rows in many])
    size = 256 * len(many)
    both = jnp.dot(jnp.concatenate(highs + lows, axis=0), right, preferred_element_type=F32)
    return both[:size] + both[size:]


def messages(total):
    for pair in range(total.shape[0] // 128):
        turned = total[128 * pair : 128 * pair + 128].T
        yield pair, turned[:64] + turned[64:]


def weighted_rows(rows_ref, field, weight, a):
    weighted = field * weight
    for block in range(16):
        rows_ref[block, 4 * a : 4 * a + 4, :] = weighted[4 * block : 4 * block + 4]


def components(ref, *at):
    return [ref[(*at, a)] for a in range(3)]


def plane_blocks(half, rows_ref, grad_ref, right_ref, out_ref):
    for block in range(0, 8, 2):
        many = [rows_ref[2 * (block + m) + half] for m in range(2)]
        total = block_sums(many, components(grad_ref, 0), right_ref[0])
        total = total + block_sums(many, components(grad_ref, 1), right_ref[1])
        for pair, sums in messages(total):
            for j in range(8):
                at, sub = 8 * (block + pair // 2) + j, slice(8 * (pair % 2), 8 * (pair % 2) + 8)
                out_ref[at, sub, :] = sums[8 * j : 8 * j + 8]


def plane_kernel(
    scale, modes_ref, weights_ref, theirs_ref, mine_ref, rows_ref, field_ref, edge_right_ref, weight_ref, grad_ref, right_ref, sems
):
    fetches = [pltpu.make_async_copy(weights_ref, weight_ref, sems.at[3])]
    fetches += [pltpu.make_async_copy(modes_ref.at[a], field_ref.at[a], sems.at[a]) for a in range(3)]
    for fetch in fetches:
        fetch.start()
    cells = field_ref.shape[2]
    lane = lax.broadcasted_iota(jnp.int32, field_ref.shape[1:], 1) % NX
    fetches[0].wait()
    weight = weight_ref[...] * scale
    for a in range(3):
        fetches[1 + a].wait()
        field = field_ref[a]
        weighted_rows(rows_ref, field, weight, a)
        after = jnp.where(lane == NX - 1, pltpu.roll(field, NX - 1, 1), pltpu.roll(field, cells - 1, 1))
        before = jnp.where(lane == 0, pltpu.roll(field, cells - (NX - 1), 1), pltpu.roll(field, 1, 1))
        grad_ref[0, a] = after - before
        grad_ref[1, a] = pltpu.roll(field, cells - NX, 1) - pltpu.roll(field, NX, 1)
        if a < 2:
            right_ref[a] = stationary(field)
        else:
            edge_right_ref[...] = stationary(field)
    core = lax.axis_index("c")
    plane_blocks(1 - core, rows_ref, grad_ref, right_ref, theirs_ref)
    plane_blocks(core, rows_ref, grad_ref, right_ref, mine_ref)


def edge_blocks(half, slope_ref, rows_ref, low_rows_ref, right_ref, low_right_ref, partial_ref, out_ref):
    slopes = components(slope_ref)
    for block in range(0, 8, 2):
        many = [2 * (block + m) + half for m in range(2)]
        total = block_sums([rows_ref[m] for m in many], slopes, right_ref[...])
        total = total + block_sums([low_rows_ref[m] for m in many], slopes, low_right_ref[...])
        for pair, sums in messages(total):
            for j in range(8):
                at, sub = 8 * (block + pair // 2) + j, slice(8 * (pair % 2), 8 * (pair % 2) + 8)
                out_ref[at, sub, :] = partial_ref[at, sub, :] + sums[8 * j : 8 * j + 8]


def first_edge_kernel(
    scale, field_ref, below_ref, weight_ref, rows_ref, right_ref, partial_ref, out_ref, slope_ref, low_rows_ref, low_right_ref
):
    weight = weight_ref[...] * scale
    for a in range(3):
        slope_ref[a] = field_ref[a] - below_ref[a]
        weighted_rows(low_rows_ref, below_ref[a], weight, a)
    low_right_ref[...] = stationary(below_ref[2])
    half = 1 - lax.axis_index("c")
    edge_blocks(half, slope_ref, rows_ref, low_rows_ref, right_ref, low_right_ref, partial_ref, out_ref)


def second_edge_kernel(slope_ref, rows_ref, low_rows_ref, right_ref, low_right_ref, partial_ref, out_ref):
    half = lax.axis_index("c")
    edge_blocks(half, slope_ref, rows_ref, low_rows_ref, right_ref, low_right_ref, partial_ref, out_ref)


def final_kernel(blocks_ref, out_ref):
    total = jnp.sum(blocks_ref[...], axis=0)
    for h in range(2):
        rows = total[8 * h : 8 * h + 8]
        out_ref[2 * h] = rows[:, :64]
        out_ref[2 * h + 1] = rows[:, 64:]


LIMIT = 12 << 20
VM = pl.BlockSpec(memory_space=pltpu.VMEM)


HBM = pl.BlockSpec(memory_space=pltpu.HBM)


def local_call(kernel, name, outs, *args, scratch=(), spec=VM):
    args = [pltpu.with_memory_space_constraint(arg, spec.memory_space) for arg in args]
    return pl.pallas_call(
        kernel,
        out_shape=[pltpu.VMEM(shape, kind) for shape, kind in outs],
        in_specs=[spec] * len(args),
        out_specs=[VM] * len(outs),
        scratch_shapes=scratch,
        compiler_params=pltpu.CompilerParams(vmem_limit_bytes=LIMIT),
        name=name,
    )(*args)


def per_device(modes, weights, *, count):
    cells = modes.shape[2]
    factor = 0.5 / math.sqrt(count * cells)
    up = [(i, (i + 1) % count) for i in range(count)]
    weights = weights.reshape(1, cells)
    below = lax.ppermute(modes, PARTS, up)
    below_weight = lax.ppermute(weights, PARTS, up)

    blocks = ((64, 16, 128), F32)
    rows_shape = ((16, 12, cells), F32)
    plane = ((3, 64, cells), F32)
    right_shape = ((cells, 128), BF16)
    theirs, mine, rows, field, right = local_call(
        functools.partial(plane_kernel, factor),
        "plane",
        [blocks, blocks, rows_shape, plane, right_shape],
        modes,
        weights,
        scratch=[
            pltpu.VMEM((1, cells), F32),
            pltpu.VMEM((2, 3, 64, cells), F32),
            pltpu.VMEM((2, cells, 128), BF16),
            pltpu.SemaphoreType.DMA((4,)),
        ],
        spec=HBM,
    )
    theirs, slope, low_rows, low_right = local_call(
        functools.partial(first_edge_kernel, factor),
        "edge_theirs",
        [blocks, plane, rows_shape, right_shape],
        field,
        below,
        below_weight,
        rows,
        right,
        theirs,
    )
    arrived = lax.ppermute(theirs, PARTS, [(i, i ^ 8) for i in range(count)])
    (mine,) = local_call(
        second_edge_kernel, "edge_mine", [blocks], slope, rows, low_rows, right, low_right, mine
    )
    gathered = lax.all_to_all(mine + arrived, CHIPS, split_axis=0, concat_axis=0, tiled=True)
    return pl.pallas_call(
        final_kernel, out_shape=jax.ShapeDtypeStruct((4, 8, 64), F32), in_specs=[VM], out_specs=VM, name="final"
    )(pltpu.with_memory_space_constraint(gathered, pltpu.VMEM))


def solution(mesh):
    fine = Mesh(np.asarray(mesh.devices).reshape(4, 2, 2, 2, 4), PARTS)
    return jax.shard_map(
        functools.partial(per_device, count=mesh.devices.size),
        mesh=fine,
        in_specs=(P(None, None, PARTS), P(PARTS)),
        out_specs=P(("x", "yh", "c"), ("yl", "z"), None),
        check_vma=False,
    )
```

```python
import functools
import math

import numpy as np
import jax
import jax.numpy as jnp
from jax import lax
from jax.experimental import pallas as pl
from jax.experimental.pallas import tpu as pltpu
from jax.sharding import Mesh, PartitionSpec as P

NX = 16
PARTS = ("x", "yh", "c", "yl", "z")
CHIPS = ("x", "yh", "yl", "z")
F32 = jnp.float32
BF16 = jnp.bfloat16


def halves(value):
    high = value.astype(BF16)
    low = (value - high.astype(F32)).astype(BF16)
    return high, low


def stationary(field):
    tall = jnp.concatenate([field, field], axis=0).T
    high = tall.astype(BF16).astype(F32)
    first = lax.broadcasted_iota(jnp.int32, tall.shape, 1) < field.shape[0]
    return jnp.where(first, high, tall - high).astype(BF16)


def products(rows, grads):
    pieces = []
    for i in range(4):
        inner = rows[i : i + 1] * grads[0]
        inner = inner + rows[4 + i : 5 + i] * grads[1]
        inner = inner + rows[8 + i : 9 + i] * grads[2]
        pieces.append(inner)
    return halves(jnp.concatenate(pieces, axis=0))


def block_sums(many, grads, right):
    highs, lows = zip(*[products(rows, grads) for rows in many])
    size = 256 * len(many)
    both = jnp.dot(jnp.concatenate(highs + lows, axis=0), right, preferred_element_type=F32)
    return both[:size] + both[size:]


def joined_sums(many, low_many, grads, low_grads, right, low_right):
    lefts = []
    for rows, low_rows in zip(many, low_many):
        high, low = products(rows, grads)
        low_high, low_low = products(low_rows, low_grads)
        lefts.append(jnp.concatenate([high, low_high], axis=1))
        lefts.append(jnp.concatenate([low, low_low], axis=1))
    size = 256
    both = jnp.dot(jnp.concatenate(lefts, axis=0), jnp.concatenate([right, low_right], axis=0), preferred_element_type=F32)
    return jnp.concatenate([both[2 * size * m : 2 * size * m + size] + both[2 * size * m + size : 2 * size * (m + 1)] for m in range(len(many))], axis=0)


def messages(total):
    for pair in range(total.shape[0] // 128):
        turned = total[128 * pair : 128 * pair + 128].T
        yield pair, turned[:64] + turned[64:]


def weighted_rows(rows_ref, field, weight, a):
    weighted = field * weight
    for block in range(16):
        rows_ref[block, 4 * a : 4 * a + 4, :] = weighted[4 * block : 4 * block + 4]


def components(ref, *at):
    return [ref[(*at, a)] for a in range(3)]


def plane_blocks(half, rows_ref, grad_ref, right_ref, out_ref):
    for block in range(0, 8, 2):
        many = [rows_ref[2 * (block + m) + half] for m in range(2)]
        total = joined_sums(many, many, components(grad_ref, 0), components(grad_ref, 1), right_ref[0], right_ref[1])
        for pair, sums in messages(total):
            for j in range(8):
                at, sub = 8 * (block + pair // 2) + j, slice(8 * (pair % 2), 8 * (pair % 2) + 8)
                out_ref[at, sub, :] = sums[8 * j : 8 * j + 8]


def plane_kernel(
    scale, modes_ref, weights_ref, theirs_ref, mine_ref, rows_ref, field_ref, edge_right_ref, weight_ref, grad_ref, right_ref, sems
):
    fetches = [pltpu.make_async_copy(weights_ref, weight_ref, sems.at[3])]
    fetches += [pltpu.make_async_copy(modes_ref.at[a], field_ref.at[a], sems.at[a]) for a in range(3)]
    for fetch in fetches:
        fetch.start()
    cells = field_ref.shape[2]
    lane = lax.broadcasted_iota(jnp.int32, field_ref.shape[1:], 1) % NX
    fetches[0].wait()
    weight = weight_ref[...] * scale
    for a in range(3):
        fetches[1 + a].wait()
        field = field_ref[a]
        weighted_rows(rows_ref, field, weight, a)
        after = jnp.where(lane == NX - 1, pltpu.roll(field, NX - 1, 1), pltpu.roll(field, cells - 1, 1))
        before = jnp.where(lane == 0, pltpu.roll(field, cells - (NX - 1), 1), pltpu.roll(field, 1, 1))
        grad_ref[0, a] = after - before
        grad_ref[1, a] = pltpu.roll(field, cells - NX, 1) - pltpu.roll(field, NX, 1)
        if a < 2:
            right_ref[a] = stationary(field)
        else:
            edge_right_ref[...] = stationary(field)
    core = lax.axis_index("c")
    plane_blocks(1 - core, rows_ref, grad_ref, right_ref, theirs_ref)
    plane_blocks(core, rows_ref, grad_ref, right_ref, mine_ref)


def edge_blocks(half, slope_ref, rows_ref, low_rows_ref, right_ref, low_right_ref, partial_ref, out_ref):
    slopes = components(slope_ref)
    for block in range(0, 8, 2):
        many = [2 * (block + m) + half for m in range(2)]
        total = joined_sums([rows_ref[m] for m in many], [low_rows_ref[m] for m in many], slopes, slopes, right_ref[...], low_right_ref[...])
        for pair, sums in messages(total):
            for j in range(8):
                at, sub = 8 * (block + pair // 2) + j, slice(8 * (pair % 2), 8 * (pair % 2) + 8)
                out_ref[at, sub, :] = partial_ref[at, sub, :] + sums[8 * j : 8 * j + 8]


def first_edge_kernel(
    scale, field_ref, below_ref, weight_ref, rows_ref, right_ref, partial_ref, out_ref, slope_ref, low_rows_ref, low_right_ref
):
    weight = weight_ref[...] * scale
    for a in range(3):
        slope_ref[a] = field_ref[a] - below_ref[a]
        weighted_rows(low_rows_ref, below_ref[a], weight, a)
    low_right_ref[...] = stationary(below_ref[2])
    half = 1 - lax.axis_index("c")
    edge_blocks(half, slope_ref, rows_ref, low_rows_ref, right_ref, low_right_ref, partial_ref, out_ref)


def second_edge_kernel(slope_ref, rows_ref, low_rows_ref, right_ref, low_right_ref, partial_ref, out_ref):
    half = lax.axis_index("c")
    edge_blocks(half, slope_ref, rows_ref, low_rows_ref, right_ref, low_right_ref, partial_ref, out_ref)


def final_kernel(blocks_ref, out_ref):
    groups = [blocks_ref[8 * g : 8 * g + 8] for g in range(8)]
    while len(groups) > 1:
        groups = [a + b for a, b in zip(groups[::2], groups[1::2])]
    total = jnp.sum(groups[0], axis=0)
    for h in range(2):
        rows = total[8 * h : 8 * h + 8]
        out_ref[2 * h] = rows[:, :64]
        out_ref[2 * h + 1] = rows[:, 64:]


LIMIT = 12 << 20
VM = pl.BlockSpec(memory_space=pltpu.VMEM)


HBM = pl.BlockSpec(memory_space=pltpu.HBM)


def local_call(kernel, name, outs, *args, scratch=(), spec=VM):
    args = [pltpu.with_memory_space_constraint(arg, spec.memory_space) for arg in args]
    return pl.pallas_call(
        kernel,
        out_shape=[pltpu.VMEM(shape, kind) for shape, kind in outs],
        in_specs=[spec] * len(args),
        out_specs=[VM] * len(outs),
        scratch_shapes=scratch,
        compiler_params=pltpu.CompilerParams(vmem_limit_bytes=LIMIT),
        name=name,
    )(*args)


def per_device(modes, weights, *, count):
    cells = modes.shape[2]
    factor = 0.5 / math.sqrt(count * cells)
    up = [(i, (i + 1) % count) for i in range(count)]
    weights = weights.reshape(1, cells)
    below = lax.ppermute(modes, PARTS, up)
    below_weight = lax.ppermute(weights, PARTS, up)

    blocks = ((64, 16, 128), F32)
    rows_shape = ((16, 12, cells), F32)
    plane = ((3, 64, cells), F32)
    right_shape = ((cells, 128), BF16)
    theirs, mine, rows, field, right = local_call(
        functools.partial(plane_kernel, factor),
        "plane",
        [blocks, blocks, rows_shape, plane, right_shape],
        modes,
        weights,
        scratch=[
            pltpu.VMEM((1, cells), F32),
            pltpu.VMEM((2, 3, 64, cells), F32),
            pltpu.VMEM((2, cells, 128), BF16),
            pltpu.SemaphoreType.DMA((4,)),
        ],
        spec=HBM,
    )
    theirs, slope, low_rows, low_right = local_call(
        functools.partial(first_edge_kernel, factor),
        "edge_theirs",
        [blocks, plane, rows_shape, right_shape],
        field,
        below,
        below_weight,
        rows,
        right,
        theirs,
    )
    arrived = lax.ppermute(theirs, PARTS, [(i, i ^ 8) for i in range(count)])
    (mine,) = local_call(
        second_edge_kernel, "edge_mine", [blocks], slope, rows, low_rows, right, low_right, mine
    )
    gathered = lax.all_to_all(mine + arrived, CHIPS, split_axis=0, concat_axis=0, tiled=True)
    return pl.pallas_call(
        final_kernel, out_shape=jax.ShapeDtypeStruct((4, 8, 64), F32), in_specs=[VM], out_specs=VM, name="final"
    )(pltpu.with_memory_space_constraint(gathered, pltpu.VMEM))


def solution(mesh):
    fine = Mesh(np.asarray(mesh.devices).reshape(4, 2, 2, 2, 4), PARTS)
    return jax.shard_map(
        functools.partial(per_device, count=mesh.devices.size),
        mesh=fine,
        in_specs=(P(None, None, PARTS), P(PARTS)),
        out_specs=P(("x", "yh", "c"), ("yl", "z"), None),
        check_vma=False,
    )
```

```python
import functools
import math

import numpy as np
import jax
import jax.numpy as jnp
from jax import lax
from jax.experimental import pallas as pl
from jax.experimental.pallas import tpu as pltpu
from jax.sharding import Mesh, PartitionSpec as P

NX = 16
PARTS = ("x", "yh", "c", "yl", "z")
CHIPS = ("x", "yh", "yl", "z")
F32 = jnp.float32
BF16 = jnp.bfloat16


def halves(value):
    high = value.astype(BF16)
    low = (value - high.astype(F32)).astype(BF16)
    return high, low


def stationary(field):
    tall = jnp.concatenate([field, field], axis=0).T
    high = tall.astype(BF16).astype(F32)
    first = lax.broadcasted_iota(jnp.int32, tall.shape, 1) < field.shape[0]
    return jnp.where(first, high, tall - high).astype(BF16)


def products(rows, grads):
    pieces = []
    for i in range(4):
        inner = rows[i : i + 1] * grads[0]
        inner = inner + rows[4 + i : 5 + i] * grads[1]
        inner = inner + rows[8 + i : 9 + i] * grads[2]
        pieces.append(inner)
    return halves(jnp.concatenate(pieces, axis=0))


def block_sums(many, grads, right):
    highs, lows = zip(*[products(rows, grads) for rows in many])
    size = 256 * len(many)
    both = jnp.dot(jnp.concatenate(highs + lows, axis=0), right, preferred_element_type=F32)
    return both[:size] + both[size:]


def joined_sums(many, low_many, grads, low_grads, right, low_right):
    lefts = []
    for rows, low_rows in zip(many, low_many):
        high, low = products(rows, grads)
        low_high, low_low = products(low_rows, low_grads)
        lefts.append(jnp.concatenate([high, low_high], axis=1))
        lefts.append(jnp.concatenate([low, low_low], axis=1))
    size = 256
    both = jnp.dot(jnp.concatenate(lefts, axis=0), jnp.concatenate([right, low_right], axis=0), preferred_element_type=F32)
    return jnp.concatenate([both[2 * size * m : 2 * size * m + size] + both[2 * size * m + size : 2 * size * (m + 1)] for m in range(len(many))], axis=0)


def messages(total):
    for pair in range(total.shape[0] // 128):
        turned = total[128 * pair : 128 * pair + 128].T
        yield pair, turned[:64] + turned[64:]


def weighted_rows(rows_ref, field, weight, a):
    weighted = field * weight
    for block in range(16):
        rows_ref[block, 4 * a : 4 * a + 4, :] = weighted[4 * block : 4 * block + 4]


def components(ref, *at):
    return [ref[(*at, a)] for a in range(3)]


def plane_blocks(half, rows_ref, grad_ref, right_ref, out_ref):
    for block in range(0, 8, 2):
        many = [rows_ref[2 * (block + m) + half] for m in range(2)]
        total = block_sums(many, components(grad_ref, 0), right_ref[0])
        total = total + block_sums(many, components(grad_ref, 1), right_ref[1])
        for pair, sums in messages(total):
            for j in range(8):
                at, sub = 8 * (block + pair // 2) + j, slice(8 * (pair % 2), 8 * (pair % 2) + 8)
                out_ref[at, sub, :] = sums[8 * j : 8 * j + 8]


def plane_kernel(
    scale, modes_ref, weights_ref, theirs_ref, mine_ref, rows_ref, field_ref, edge_right_ref, weight_ref, grad_ref, right_ref, sems
):
    fetches = [pltpu.make_async_copy(weights_ref, weight_ref, sems.at[3])]
    fetches += [pltpu.make_async_copy(modes_ref.at[a], field_ref.at[a], sems.at[a]) for a in range(3)]
    for fetch in fetches:
        fetch.start()
    cells = field_ref.shape[2]
    lane = lax.broadcasted_iota(jnp.int32, field_ref.shape[1:], 1) % NX
    fetches[0].wait()
    weight = weight_ref[...] * scale
    for a in range(3):
        fetches[1 + a].wait()
        field = field_ref[a]
        weighted_rows(rows_ref, field, weight, a)
        after = jnp.where(lane == NX - 1, pltpu.roll(field, NX - 1, 1), pltpu.roll(field, cells - 1, 1))
        before = jnp.where(lane == 0, pltpu.roll(field, cells - (NX - 1), 1), pltpu.roll(field, 1, 1))
        grad_ref[0, a] = after - before
        grad_ref[1, a] = pltpu.roll(field, cells - NX, 1) - pltpu.roll(field, NX, 1)
        if a < 2:
            right_ref[a] = stationary(field)
        else:
            edge_right_ref[...] = stationary(field)
    core = lax.axis_index("c")
    plane_blocks(1 - core, rows_ref, grad_ref, right_ref, theirs_ref)
    plane_blocks(core, rows_ref, grad_ref, right_ref, mine_ref)


def edge_blocks(half, slope_ref, rows_ref, low_rows_ref, right_ref, low_right_ref, partial_ref, out_ref):
    slopes = components(slope_ref)
    for block in range(0, 8, 2):
        many = [2 * (block + m) + half for m in range(2)]
        total = joined_sums([rows_ref[m] for m in many], [low_rows_ref[m] for m in many], slopes, slopes, right_ref[...], low_right_ref[...])
        for pair, sums in messages(total):
            for j in range(8):
                at, sub = 8 * (block + pair // 2) + j, slice(8 * (pair % 2), 8 * (pair % 2) + 8)
                out_ref[at, sub, :] = partial_ref[at, sub, :] + sums[8 * j : 8 * j + 8]


def first_edge_kernel(
    scale, field_ref, below_ref, weight_ref, rows_ref, right_ref, partial_ref, out_ref, slope_ref, low_rows_ref, low_right_ref
):
    weight = weight_ref[...] * scale
    for a in range(3):
        slope_ref[a] = field_ref[a] - below_ref[a]
        weighted_rows(low_rows_ref, below_ref[a], weight, a)
    low_right_ref[...] = stationary(below_ref[2])
    half = 1 - lax.axis_index("c")
    edge_blocks(half, slope_ref, rows_ref, low_rows_ref, right_ref, low_right_ref, partial_ref, out_ref)


def second_edge_kernel(slope_ref, rows_ref, low_rows_ref, right_ref, low_right_ref, partial_ref, out_ref):
    half = lax.axis_index("c")
    edge_blocks(half, slope_ref, rows_ref, low_rows_ref, right_ref, low_right_ref, partial_ref, out_ref)


def final_kernel(blocks_ref, out_ref):
    groups = [blocks_ref[8 * g : 8 * g + 8] for g in range(8)]
    while len(groups) > 1:
        groups = [a + b for a, b in zip(groups[::2], groups[1::2])]
    total = jnp.sum(groups[0], axis=0)
    for h in range(2):
        rows = total[8 * h : 8 * h + 8]
        out_ref[2 * h] = rows[:, :64]
        out_ref[2 * h + 1] = rows[:, 64:]


LIMIT = 12 << 20
VM = pl.BlockSpec(memory_space=pltpu.VMEM)


HBM = pl.BlockSpec(memory_space=pltpu.HBM)


def local_call(kernel, name, outs, *args, scratch=(), spec=VM):
    args = [pltpu.with_memory_space_constraint(arg, spec.memory_space) for arg in args]
    return pl.pallas_call(
        kernel,
        out_shape=[pltpu.VMEM(shape, kind) for shape, kind in outs],
        in_specs=[spec] * len(args),
        out_specs=[VM] * len(outs),
        scratch_shapes=scratch,
        compiler_params=pltpu.CompilerParams(vmem_limit_bytes=LIMIT),
        name=name,
    )(*args)


def per_device(modes, weights, *, count):
    cells = modes.shape[2]
    factor = 0.5 / math.sqrt(count * cells)
    up = [(i, (i + 1) % count) for i in range(count)]
    weights = weights.reshape(1, cells)
    below = lax.ppermute(modes, PARTS, up)
    below_weight = lax.ppermute(weights, PARTS, up)

    blocks = ((64, 16, 128), F32)
    rows_shape = ((16, 12, cells), F32)
    plane = ((3, 64, cells), F32)
    right_shape = ((cells, 128), BF16)
    theirs, mine, rows, field, right = local_call(
        functools.partial(plane_kernel, factor),
        "plane",
        [blocks, blocks, rows_shape, plane, right_shape],
        modes,
        weights,
        scratch=[
            pltpu.VMEM((1, cells), F32),
            pltpu.VMEM((2, 3, 64, cells), F32),
            pltpu.VMEM((2, cells, 128), BF16),
            pltpu.SemaphoreType.DMA((4,)),
        ],
        spec=HBM,
    )
    theirs, slope, low_rows, low_right = local_call(
        functools.partial(first_edge_kernel, factor),
        "edge_theirs",
        [blocks, plane, rows_shape, right_shape],
        field,
        below,
        below_weight,
        rows,
        right,
        theirs,
    )
    arrived = lax.ppermute(theirs, PARTS, [(i, i ^ 8) for i in range(count)])
    (mine,) = local_call(
        second_edge_kernel, "edge_mine", [blocks], slope, rows, low_rows, right, low_right, mine
    )
    gathered = lax.all_to_all(mine + arrived, CHIPS, split_axis=0, concat_axis=0, tiled=True)
    return pl.pallas_call(
        final_kernel, out_shape=jax.ShapeDtypeStruct((4, 8, 64), F32), in_specs=[VM], out_specs=VM, name="final"
    )(pltpu.with_memory_space_constraint(gathered, pltpu.VMEM))


def solution(mesh):
    fine = Mesh(np.asarray(mesh.devices).reshape(4, 2, 2, 2, 4), PARTS)
    return jax.shard_map(
        functools.partial(per_device, count=mesh.devices.size),
        mesh=fine,
        in_specs=(P(None, None, PARTS), P(PARTS)),
        out_specs=P(("x", "yh", "c"), ("yl", "z"), None),
        check_vma=False,
    )
```

```python
import functools
import math

import numpy as np
import jax
import jax.numpy as jnp
from jax import lax
from jax.experimental import pallas as pl
from jax.experimental.pallas import tpu as pltpu
from jax.sharding import Mesh, PartitionSpec as P

NX = 16
PARTS = ("x", "yh", "c", "yl", "z")
CHIPS = ("x", "yh", "yl", "z")
F32 = jnp.float32
BF16 = jnp.bfloat16


def halves(value):
    high = value.astype(BF16)
    low = (value - high.astype(F32)).astype(BF16)
    return high, low


def stationary(field):
    tall = jnp.concatenate([field, field], axis=0).T
    high = tall.astype(BF16).astype(F32)
    first = lax.broadcasted_iota(jnp.int32, tall.shape, 1) < field.shape[0]
    return jnp.where(first, high, tall - high).astype(BF16)


def products(rows, grads):
    pieces = []
    for i in range(4):
        inner = rows[i : i + 1] * grads[0]
        inner = inner + rows[4 + i : 5 + i] * grads[1]
        inner = inner + rows[8 + i : 9 + i] * grads[2]
        pieces.append(inner)
    return halves(jnp.concatenate(pieces, axis=0))


def block_sums(many, grads, right):
    highs, lows = zip(*[products(rows, grads) for rows in many])
    size = 256 * len(many)
    both = jnp.dot(jnp.concatenate(highs + lows, axis=0), right, preferred_element_type=F32)
    return both[:size] + both[size:]


def joined_sums(many, low_many, grads, low_grads, right, low_right):
    lefts = []
    for rows, low_rows in zip(many, low_many):
        high, low = products(rows, grads)
        low_high, low_low = products(low_rows, low_grads)
        lefts.append(jnp.concatenate([high, low_high], axis=1))
        lefts.append(jnp.concatenate([low, low_low], axis=1))
    size = 256
    both = jnp.dot(jnp.concatenate(lefts, axis=0), jnp.concatenate([right, low_right], axis=0), preferred_element_type=F32)
    return jnp.concatenate([both[2 * size * m : 2 * size * m + size] + both[2 * size * m + size : 2 * size * (m + 1)] for m in range(len(many))], axis=0)


def messages(total):
    for pair in range(total.shape[0] // 128):
        turned = total[128 * pair : 128 * pair + 128].T
        yield pair, turned[:64] + turned[64:]


def weighted_rows(rows_ref, field, weight, a):
    weighted = field * weight
    for block in range(16):
        rows_ref[block, 4 * a : 4 * a + 4, :] = weighted[4 * block : 4 * block + 4]


def components(ref, *at):
    return [ref[(*at, a)] for a in range(3)]


def plane_blocks(half, rows_ref, grad_ref, right_ref, out_ref):
    for block in range(0, 8, 4):
        many = [rows_ref[2 * (block + m) + half] for m in range(4)]
        total = block_sums(many, components(grad_ref, 0), right_ref[0])
        total = total + block_sums(many, components(grad_ref, 1), right_ref[1])
        for pair, sums in messages(total):
            for j in range(8):
                at, sub = 8 * (block + pair // 2) + j, slice(8 * (pair % 2), 8 * (pair % 2) + 8)
                out_ref[at, sub, :] = sums[8 * j : 8 * j + 8]


def plane_kernel(
    scale, modes_ref, weights_ref, theirs_ref, mine_ref, rows_ref, field_ref, edge_right_ref, weight_ref, grad_ref, right_ref, sems
):
    fetches = [pltpu.make_async_copy(weights_ref, weight_ref, sems.at[3])]
    fetches += [pltpu.make_async_copy(modes_ref.at[a], field_ref.at[a], sems.at[a]) for a in range(3)]
    for fetch in fetches:
        fetch.start()
    cells = field_ref.shape[2]
    lane = lax.broadcasted_iota(jnp.int32, field_ref.shape[1:], 1) % NX
    fetches[0].wait()
    weight = weight_ref[...] * scale
    for a in range(3):
        fetches[1 + a].wait()
        field = field_ref[a]
        weighted_rows(rows_ref, field, weight, a)
        after = jnp.where(lane == NX - 1, pltpu.roll(field, NX - 1, 1), pltpu.roll(field, cells - 1, 1))
        before = jnp.where(lane == 0, pltpu.roll(field, cells - (NX - 1), 1), pltpu.roll(field, 1, 1))
        grad_ref[0, a] = after - before
        grad_ref[1, a] = pltpu.roll(field, cells - NX, 1) - pltpu.roll(field, NX, 1)
        if a < 2:
            right_ref[a] = stationary(field)
        else:
            edge_right_ref[...] = stationary(field)
    core = lax.axis_index("c")
    plane_blocks(1 - core, rows_ref, grad_ref, right_ref, theirs_ref)
    plane_blocks(core, rows_ref, grad_ref, right_ref, mine_ref)


def edge_blocks(half, slope_ref, rows_ref, low_rows_ref, right_ref, low_right_ref, partial_ref, out_ref):
    slopes = components(slope_ref)
    for block in range(0, 8, 4):
        many = [2 * (block + m) + half for m in range(4)]
        total = joined_sums([rows_ref[m] for m in many], [low_rows_ref[m] for m in many], slopes, slopes, right_ref[...], low_right_ref[...])
        for pair, sums in messages(total):
            for j in range(8):
                at, sub = 8 * (block + pair // 2) + j, slice(8 * (pair % 2), 8 * (pair % 2) + 8)
                out_ref[at, sub, :] = partial_ref[at, sub, :] + sums[8 * j : 8 * j + 8]


def first_edge_kernel(
    scale, field_ref, below_ref, weight_ref, rows_ref, right_ref, partial_ref, out_ref, slope_ref, low_rows_ref, low_right_ref
):
    weight = weight_ref[...] * scale
    for a in range(3):
        slope_ref[a] = field_ref[a] - below_ref[a]
        weighted_rows(low_rows_ref, below_ref[a], weight, a)
    low_right_ref[...] = stationary(below_ref[2])
    half = 1 - lax.axis_index("c")
    edge_blocks(half, slope_ref, rows_ref, low_rows_ref, right_ref, low_right_ref, partial_ref, out_ref)


def second_edge_kernel(slope_ref, rows_ref, low_rows_ref, right_ref, low_right_ref, partial_ref, out_ref):
    half = lax.axis_index("c")
    edge_blocks(half, slope_ref, rows_ref, low_rows_ref, right_ref, low_right_ref, partial_ref, out_ref)


def final_kernel(blocks_ref, out_ref):
    groups = [blocks_ref[8 * g : 8 * g + 8] for g in range(8)]
    while len(groups) > 1:
        groups = [a + b for a, b in zip(groups[::2], groups[1::2])]
    total = jnp.sum(groups[0], axis=0)
    for h in range(2):
        rows = total[8 * h : 8 * h + 8]
        out_ref[2 * h] = rows[:, :64]
        out_ref[2 * h + 1] = rows[:, 64:]


LIMIT = 12 << 20
VM = pl.BlockSpec(memory_space=pltpu.VMEM)


HBM = pl.BlockSpec(memory_space=pltpu.HBM)


def local_call(kernel, name, outs, *args, scratch=(), spec=VM):
    args = [pltpu.with_memory_space_constraint(arg, spec.memory_space) for arg in args]
    return pl.pallas_call(
        kernel,
        out_shape=[pltpu.VMEM(shape, kind) for shape, kind in outs],
        in_specs=[spec] * len(args),
        out_specs=[VM] * len(outs),
        scratch_shapes=scratch,
        compiler_params=pltpu.CompilerParams(vmem_limit_bytes=LIMIT),
        name=name,
    )(*args)


def per_device(modes, weights, *, count):
    cells = modes.shape[2]
    factor = 0.5 / math.sqrt(count * cells)
    up = [(i, (i + 1) % count) for i in range(count)]
    weights = weights.reshape(1, cells)
    below = lax.ppermute(modes, PARTS, up)
    below_weight = lax.ppermute(weights, PARTS, up)

    blocks = ((64, 16, 128), F32)
    rows_shape = ((16, 12, cells), F32)
    plane = ((3, 64, cells), F32)
    right_shape = ((cells, 128), BF16)
    theirs, mine, rows, field, right = local_call(
        functools.partial(plane_kernel, factor),
        "plane",
        [blocks, blocks, rows_shape, plane, right_shape],
        modes,
        weights,
        scratch=[
            pltpu.VMEM((1, cells), F32),
            pltpu.VMEM((2, 3, 64, cells), F32),
            pltpu.VMEM((2, cells, 128), BF16),
            pltpu.SemaphoreType.DMA((4,)),
        ],
        spec=HBM,
    )
    theirs, slope, low_rows, low_right = local_call(
        functools.partial(first_edge_kernel, factor),
        "edge_theirs",
        [blocks, plane, rows_shape, right_shape],
        field,
        below,
        below_weight,
        rows,
        right,
        theirs,
    )
    arrived = lax.ppermute(theirs, PARTS, [(i, i ^ 8) for i in range(count)])
    (mine,) = local_call(
        second_edge_kernel, "edge_mine", [blocks], slope, rows, low_rows, right, low_right, mine
    )
    gathered = lax.all_to_all(mine + arrived, CHIPS, split_axis=0, concat_axis=0, tiled=True)
    return pl.pallas_call(
        final_kernel, out_shape=jax.ShapeDtypeStruct((4, 8, 64), F32), in_specs=[VM], out_specs=VM, name="final"
    )(pltpu.with_memory_space_constraint(gathered, pltpu.VMEM))


def solution(mesh):
    fine = Mesh(np.asarray(mesh.devices).reshape(4, 2, 2, 2, 4), PARTS)
    return jax.shard_map(
        functools.partial(per_device, count=mesh.devices.size),
        mesh=fine,
        in_specs=(P(None, None, PARTS), P(PARTS)),
        out_specs=P(("x", "yh", "c"), ("yl", "z"), None),
        check_vma=False,
    )
```

```python
import functools
import math

import numpy as np
import jax
import jax.numpy as jnp
from jax import lax
from jax.experimental import pallas as pl
from jax.experimental.pallas import tpu as pltpu
from jax.sharding import Mesh, PartitionSpec as P

NX = 16
PARTS = ("x", "yh", "c", "yl", "z")
CHIPS = ("x", "yh", "yl", "z")
F32 = jnp.float32
BF16 = jnp.bfloat16


def halves(value):
    high = value.astype(BF16)
    low = (value - high.astype(F32)).astype(BF16)
    return high, low


def stationary(field):
    tall = jnp.concatenate([field, field], axis=0).T
    high = tall.astype(BF16).astype(F32)
    first = lax.broadcasted_iota(jnp.int32, tall.shape, 1) < field.shape[0]
    return jnp.where(first, high, tall - high).astype(BF16)


def products(rows, grads):
    pieces = []
    for i in range(4):
        inner = rows[i : i + 1] * grads[0]
        inner = inner + rows[4 + i : 5 + i] * grads[1]
        inner = inner + rows[8 + i : 9 + i] * grads[2]
        pieces.append(inner)
    return halves(jnp.concatenate(pieces, axis=0))


def block_sums(many, grads, right):
    highs, lows = zip(*[products(rows, grads) for rows in many])
    size = 256 * len(many)
    both = jnp.dot(jnp.concatenate(highs + lows, axis=0), right, preferred_element_type=F32)
    return both[:size] + both[size:]


def joined_sums(many, low_many, grads, low_grads, right, low_right):
    lefts = []
    for rows, low_rows in zip(many, low_many):
        high, low = products(rows, grads)
        low_high, low_low = products(low_rows, low_grads)
        lefts.append(jnp.concatenate([high, low_high], axis=1))
        lefts.append(jnp.concatenate([low, low_low], axis=1))
    size = 256
    both = jnp.dot(jnp.concatenate(lefts, axis=0), jnp.concatenate([right, low_right], axis=0), preferred_element_type=F32)
    return jnp.concatenate([both[2 * size * m : 2 * size * m + size] + both[2 * size * m + size : 2 * size * (m + 1)] for m in range(len(many))], axis=0)


def messages(total):
    for pair in range(total.shape[0] // 128):
        turned = total[128 * pair : 128 * pair + 128].T
        yield pair, turned[:64] + turned[64:]


def weighted_rows(rows_ref, field, weight, a):
    weighted = field * weight
    for block in range(16):
        rows_ref[block, 4 * a : 4 * a + 4, :] = weighted[4 * block : 4 * block + 4]


def components(ref, *at):
    return [ref[(*at, a)] for a in range(3)]


def plane_blocks(half, rows_ref, grad_ref, right_ref, out_ref):
    for block in range(0, 8, 2):
        many = [rows_ref[2 * (block + m) + half] for m in range(2)]
        total = block_sums(many, components(grad_ref, 0), right_ref[0])
        total = total + block_sums(many, components(grad_ref, 1), right_ref[1])
        for pair, sums in messages(total):
            for j in range(8):
                at, sub = 8 * (block + pair // 2) + j, slice(8 * (pair % 2), 8 * (pair % 2) + 8)
                out_ref[at, sub, :] = sums[8 * j : 8 * j + 8]


def plane_kernel(
    scale, modes_ref, weights_ref, theirs_ref, mine_ref, rows_ref, field_ref, edge_right_ref, weight_ref, grad_ref, right_ref, sems
):
    fetches = [pltpu.make_async_copy(weights_ref, weight_ref, sems.at[3])]
    fetches += [pltpu.make_async_copy(modes_ref.at[a], field_ref.at[a], sems.at[a]) for a in range(3)]
    for fetch in fetches[1:] + fetches[:1]:
        fetch.start()
    cells = field_ref.shape[2]
    lane = lax.broadcasted_iota(jnp.int32, field_ref.shape[1:], 1) % NX
    fetches[0].wait()
    weight = weight_ref[...] * scale
    for a in range(3):
        fetches[1 + a].wait()
        field = field_ref[a]
        weighted_rows(rows_ref, field, weight, a)
        after = jnp.where(lane == NX - 1, pltpu.roll(field, NX - 1, 1), pltpu.roll(field, cells - 1, 1))
        before = jnp.where(lane == 0, pltpu.roll(field, cells - (NX - 1), 1), pltpu.roll(field, 1, 1))
        grad_ref[0, a] = after - before
        grad_ref[1, a] = pltpu.roll(field, cells - NX, 1) - pltpu.roll(field, NX, 1)
        if a < 2:
            right_ref[a] = stationary(field)
        else:
            edge_right_ref[...] = stationary(field)
    core = lax.axis_index("c")
    plane_blocks(1 - core, rows_ref, grad_ref, right_ref, theirs_ref)
    plane_blocks(core, rows_ref, grad_ref, right_ref, mine_ref)


def edge_blocks(half, slope_ref, rows_ref, low_rows_ref, right_ref, low_right_ref, partial_ref, out_ref):
    slopes = components(slope_ref)
    for block in range(0, 8, 2):
        many = [2 * (block + m) + half for m in range(2)]
        total = joined_sums([rows_ref[m] for m in many], [low_rows_ref[m] for m in many], slopes, slopes, right_ref[...], low_right_ref[...])
        for pair, sums in messages(total):
            for j in range(8):
                at, sub = 8 * (block + pair // 2) + j, slice(8 * (pair % 2), 8 * (pair % 2) + 8)
                out_ref[at, sub, :] = partial_ref[at, sub, :] + sums[8 * j : 8 * j + 8]


def first_edge_kernel(
    scale, field_ref, below_ref, weight_ref, rows_ref, right_ref, partial_ref, out_ref, slope_ref, low_rows_ref, low_right_ref
):
    weight = weight_ref[...] * scale
    for a in range(3):
        slope_ref[a] = field_ref[a] - below_ref[a]
        weighted_rows(low_rows_ref, below_ref[a], weight, a)
    low_right_ref[...] = stationary(below_ref[2])
    half = 1 - lax.axis_index("c")
    edge_blocks(half, slope_ref, rows_ref, low_rows_ref, right_ref, low_right_ref, partial_ref, out_ref)


def second_edge_kernel(slope_ref, rows_ref, low_rows_ref, right_ref, low_right_ref, partial_ref, out_ref):
    half = lax.axis_index("c")
    edge_blocks(half, slope_ref, rows_ref, low_rows_ref, right_ref, low_right_ref, partial_ref, out_ref)


def final_kernel(blocks_ref, out_ref):
    groups = [blocks_ref[8 * g : 8 * g + 8] for g in range(8)]
    while len(groups) > 1:
        groups = [a + b for a, b in zip(groups[::2], groups[1::2])]
    total = jnp.sum(groups[0], axis=0)
    for h in range(2):
        rows = total[8 * h : 8 * h + 8]
        out_ref[2 * h] = rows[:, :64]
        out_ref[2 * h + 1] = rows[:, 64:]


LIMIT = 12 << 20
VM = pl.BlockSpec(memory_space=pltpu.VMEM)


HBM = pl.BlockSpec(memory_space=pltpu.HBM)


def local_call(kernel, name, outs, *args, scratch=(), spec=VM):
    args = [pltpu.with_memory_space_constraint(arg, spec.memory_space) for arg in args]
    return pl.pallas_call(
        kernel,
        out_shape=[pltpu.VMEM(shape, kind) for shape, kind in outs],
        in_specs=[spec] * len(args),
        out_specs=[VM] * len(outs),
        scratch_shapes=scratch,
        compiler_params=pltpu.CompilerParams(vmem_limit_bytes=LIMIT),
        name=name,
    )(*args)


def per_device(modes, weights, *, count):
    cells = modes.shape[2]
    factor = 0.5 / math.sqrt(count * cells)
    up = [(i, (i + 1) % count) for i in range(count)]
    weights = weights.reshape(1, cells)
    below = lax.ppermute(modes, PARTS, up)
    below_weight = lax.ppermute(weights, PARTS, up)

    blocks = ((64, 16, 128), F32)
    rows_shape = ((16, 12, cells), F32)
    plane = ((3, 64, cells), F32)
    right_shape = ((cells, 128), BF16)
    theirs, mine, rows, field, right = local_call(
        functools.partial(plane_kernel, factor),
        "plane",
        [blocks, blocks, rows_shape, plane, right_shape],
        modes,
        weights,
        scratch=[
            pltpu.VMEM((1, cells), F32),
            pltpu.VMEM((2, 3, 64, cells), F32),
            pltpu.VMEM((2, cells, 128), BF16),
            pltpu.SemaphoreType.DMA((4,)),
        ],
        spec=HBM,
    )
    theirs, slope, low_rows, low_right = local_call(
        functools.partial(first_edge_kernel, factor),
        "edge_theirs",
        [blocks, plane, rows_shape, right_shape],
        field,
        below,
        below_weight,
        rows,
        right,
        theirs,
    )
    arrived = lax.ppermute(theirs, PARTS, [(i, i ^ 8) for i in range(count)])
    (mine,) = local_call(
        second_edge_kernel, "edge_mine", [blocks], slope, rows, low_rows, right, low_right, mine
    )
    gathered = lax.all_to_all(mine + arrived, CHIPS, split_axis=0, concat_axis=0, tiled=True)
    return pl.pallas_call(
        final_kernel, out_shape=jax.ShapeDtypeStruct((4, 8, 64), F32), in_specs=[VM], out_specs=VM, name="final"
    )(pltpu.with_memory_space_constraint(gathered, pltpu.VMEM))


def solution(mesh):
    fine = Mesh(np.asarray(mesh.devices).reshape(4, 2, 2, 2, 4), PARTS)
    return jax.shard_map(
        functools.partial(per_device, count=mesh.devices.size),
        mesh=fine,
        in_specs=(P(None, None, PARTS), P(PARTS)),
        out_specs=P(("x", "yh", "c"), ("yl", "z"), None),
        check_vma=False,
    )
```

```python
import functools
import math

import numpy as np
import jax
import jax.numpy as jnp
from jax import lax
from jax.experimental import pallas as pl
from jax.experimental.pallas import tpu as pltpu
from jax.sharding import Mesh, PartitionSpec as P

NX = 16
PARTS = ("x", "yh", "c", "yl", "z")
CHIPS = ("x", "yh", "yl", "z")
F32 = jnp.float32
BF16 = jnp.bfloat16


def halves(value):
    high = value.astype(BF16)
    low = (value - high.astype(F32)).astype(BF16)
    return high, low


def stationary(field):
    tall = jnp.concatenate([field, field], axis=0).T
    high = tall.astype(BF16).astype(F32)
    first = lax.broadcasted_iota(jnp.int32, tall.shape, 1) < field.shape[0]
    return jnp.where(first, high, tall - high).astype(BF16)


def products(rows, grads):
    pieces = []
    for i in range(4):
        inner = rows[i : i + 1] * grads[0]
        inner = inner + rows[4 + i : 5 + i] * grads[1]
        inner = inner + rows[8 + i : 9 + i] * grads[2]
        pieces.append(inner)
    return halves(jnp.concatenate(pieces, axis=0))


def block_sums(many, grads, right):
    highs, lows = zip(*[products(rows, grads) for rows in many])
    size = 256 * len(many)
    both = jnp.dot(jnp.concatenate(highs + lows, axis=0), right, preferred_element_type=F32)
    return both[:size] + both[size:]


def joined_sums(many, low_many, grads, low_grads, right, low_right):
    lefts = []
    for rows, low_rows in zip(many, low_many):
        high, low = products(rows, grads)
        low_high, low_low = products(low_rows, low_grads)
        lefts.append(jnp.concatenate([high, low_high], axis=1))
        lefts.append(jnp.concatenate([low, low_low], axis=1))
    size = 256
    both = jnp.dot(jnp.concatenate(lefts, axis=0), jnp.concatenate([right, low_right], axis=0), preferred_element_type=F32)
    return jnp.concatenate([both[2 * size * m : 2 * size * m + size] + both[2 * size * m + size : 2 * size * (m + 1)] for m in range(len(many))], axis=0)


def messages(total):
    for pair in range(total.shape[0] // 128):
        turned = total[128 * pair : 128 * pair + 128].T
        yield pair, turned[:64] + turned[64:]


def weighted_rows(rows_ref, field, weight, a):
    weighted = field * weight
    for block in range(16):
        rows_ref[block, 4 * a : 4 * a + 4, :] = weighted[4 * block : 4 * block + 4]


def components(ref, *at):
    return [ref[(*at, a)] for a in range(3)]


def plane_blocks(half, rows_ref, grad_ref, right_ref, out_ref):
    for block in range(0, 8, 4):
        many = [rows_ref[2 * (block + m) + half] for m in range(4)]
        total = block_sums(many, components(grad_ref, 0), right_ref[0])
        total = total + block_sums(many, components(grad_ref, 1), right_ref[1])
        for pair, sums in messages(total):
            for j in range(8):
                at, sub = 8 * (block + pair // 2) + j, slice(8 * (pair % 2), 8 * (pair % 2) + 8)
                out_ref[at, sub, :] = sums[8 * j : 8 * j + 8]


def plane_kernel(
    scale, modes_ref, weights_ref, theirs_ref, mine_ref, rows_ref, field_ref, edge_right_ref, weight_ref, grad_ref, right_ref, sems
):
    fetches = [pltpu.make_async_copy(weights_ref, weight_ref, sems.at[3])]
    fetches += [pltpu.make_async_copy(modes_ref.at[a], field_ref.at[a], sems.at[a]) for a in range(3)]
    for fetch in fetches[1:] + fetches[:1]:
        fetch.start()
    cells = field_ref.shape[2]
    lane = lax.broadcasted_iota(jnp.int32, field_ref.shape[1:], 1) % NX
    fetches[0].wait()
    weight = weight_ref[...] * scale
    for a in range(3):
        fetches[1 + a].wait()
        field = field_ref[a]
        weighted_rows(rows_ref, field, weight, a)
        after = jnp.where(lane == NX - 1, pltpu.roll(field, NX - 1, 1), pltpu.roll(field, cells - 1, 1))
        before = jnp.where(lane == 0, pltpu.roll(field, cells - (NX - 1), 1), pltpu.roll(field, 1, 1))
        grad_ref[0, a] = after - before
        grad_ref[1, a] = pltpu.roll(field, cells - NX, 1) - pltpu.roll(field, NX, 1)
        if a < 2:
            right_ref[a] = stationary(field)
        else:
            edge_right_ref[...] = stationary(field)
    core = lax.axis_index("c")
    plane_blocks(1 - core, rows_ref, grad_ref, right_ref, theirs_ref)
    plane_blocks(core, rows_ref, grad_ref, right_ref, mine_ref)


def edge_blocks(half, slope_ref, rows_ref, low_rows_ref, right_ref, low_right_ref, partial_ref, out_ref):
    slopes = components(slope_ref)
    for block in range(0, 8, 4):
        many = [2 * (block + m) + half for m in range(4)]
        total = joined_sums([rows_ref[m] for m in many], [low_rows_ref[m] for m in many], slopes, slopes, right_ref[...], low_right_ref[...])
        for pair, sums in messages(total):
            for j in range(8):
                at, sub = 8 * (block + pair // 2) + j, slice(8 * (pair % 2), 8 * (pair % 2) + 8)
                out_ref[at, sub, :] = partial_ref[at, sub, :] + sums[8 * j : 8 * j + 8]


def first_edge_kernel(
    scale, field_ref, below_ref, weight_ref, rows_ref, right_ref, partial_ref, out_ref, slope_ref, low_rows_ref, low_right_ref
):
    weight = weight_ref[...] * scale
    for a in range(3):
        slope_ref[a] = field_ref[a] - below_ref[a]
        weighted_rows(low_rows_ref, below_ref[a], weight, a)
    low_right_ref[...] = stationary(below_ref[2])
    half = 1 - lax.axis_index("c")
    edge_blocks(half, slope_ref, rows_ref, low_rows_ref, right_ref, low_right_ref, partial_ref, out_ref)


def second_edge_kernel(slope_ref, rows_ref, low_rows_ref, right_ref, low_right_ref, partial_ref, out_ref):
    half = lax.axis_index("c")
    edge_blocks(half, slope_ref, rows_ref, low_rows_ref, right_ref, low_right_ref, partial_ref, out_ref)


def final_kernel(blocks_ref, out_ref):
    groups = [blocks_ref[8 * g : 8 * g + 8] for g in range(8)]
    while len(groups) > 1:
        groups = [a + b for a, b in zip(groups[::2], groups[1::2])]
    total = jnp.sum(groups[0], axis=0)
    for h in range(2):
        rows = total[8 * h : 8 * h + 8]
        out_ref[2 * h] = rows[:, :64]
        out_ref[2 * h + 1] = rows[:, 64:]


LIMIT = 12 << 20
VM = pl.BlockSpec(memory_space=pltpu.VMEM)


HBM = pl.BlockSpec(memory_space=pltpu.HBM)


def local_call(kernel, name, outs, *args, scratch=(), spec=VM):
    args = [pltpu.with_memory_space_constraint(arg, spec.memory_space) for arg in args]
    return pl.pallas_call(
        kernel,
        out_shape=[pltpu.VMEM(shape, kind) for shape, kind in outs],
        in_specs=[spec] * len(args),
        out_specs=[VM] * len(outs),
        scratch_shapes=scratch,
        compiler_params=pltpu.CompilerParams(vmem_limit_bytes=LIMIT),
        name=name,
    )(*args)


def per_device(modes, weights, *, count):
    cells = modes.shape[2]
    factor = 0.5 / math.sqrt(count * cells)
    up = [(i, (i + 1) % count) for i in range(count)]
    weights = weights.reshape(1, cells)
    below = lax.ppermute(modes, PARTS, up)
    below_weight = lax.ppermute(weights, PARTS, up)

    blocks = ((64, 16, 128), F32)
    rows_shape = ((16, 12, cells), F32)
    plane = ((3, 64, cells), F32)
    right_shape = ((cells, 128), BF16)
    theirs, mine, rows, field, right = local_call(
        functools.partial(plane_kernel, factor),
        "plane",
        [blocks, blocks, rows_shape, plane, right_shape],
        modes,
        weights,
        scratch=[
            pltpu.VMEM((1, cells), F32),
            pltpu.VMEM((2, 3, 64, cells), F32),
            pltpu.VMEM((2, cells, 128), BF16),
            pltpu.SemaphoreType.DMA((4,)),
        ],
        spec=HBM,
    )
    theirs, slope, low_rows, low_right = local_call(
        functools.partial(first_edge_kernel, factor),
        "edge_theirs",
        [blocks, plane, rows_shape, right_shape],
        field,
        below,
        below_weight,
        rows,
        right,
        theirs,
    )
    arrived = lax.ppermute(theirs, PARTS, [(i, i ^ 8) for i in range(count)])
    (mine,) = local_call(
        second_edge_kernel, "edge_mine", [blocks], slope, rows, low_rows, right, low_right, mine
    )
    gathered = lax.all_to_all(mine + arrived, CHIPS, split_axis=0, concat_axis=0, tiled=True)
    return pl.pallas_call(
        final_kernel, out_shape=jax.ShapeDtypeStruct((4, 8, 64), F32), in_specs=[VM], out_specs=VM, name="final"
    )(pltpu.with_memory_space_constraint(gathered, pltpu.VMEM))


def solution(mesh):
    fine = Mesh(np.asarray(mesh.devices).reshape(4, 2, 2, 2, 4), PARTS)
    return jax.shard_map(
        functools.partial(per_device, count=mesh.devices.size),
        mesh=fine,
        in_specs=(P(None, None, PARTS), P(PARTS)),
        out_specs=P(("x", "yh", "c"), ("yl", "z"), None),
        check_vma=False,
    )
```
